32 devices in a mesh: tm: 4 (over z), feat: 8 (over y, x, core).
Axes of the slice: x: 2, y: 2, z: 4, core: 2. Of those that a mesh axis runs over, the one named last changes fastest.
Arguments:
- trajectory: float32 [16384, 2048], P('tm', 'feat'), may hold values from -8 to 9
Outputs:
- moments: float32 [4, 2048, 2048], P(None, 'feat', 'tm')
The draws below stay inside these ranges and needn't reach their ends.
All inputs are finite; a program needn't handle non-finite values.
Results may differ from the reference program's by a relative error of at most 0.00035.
Values may be sent and summed in bfloat16 or wider, within the bound.
No kernel may reach another device: no remote copies, remote signals or barrier semaphores. Data moves between devices by JAX's collectives and lax.ppermute only.
A program may use at most 128 MiB of HBM per device.

```python
import math
import jax
import jax.numpy as jnp
from jax import lax

F = 2048
FRAMES = 16384


def draw_trajectory(key, part):
    keys = jax.random.split(key, 8)
    times = jnp.arange(FRAMES, dtype=jnp.float32)[:, None]
    low = math.log(2.0 * math.pi / 3000.0)
    high = math.log(2.0 * math.pi / 24.0)
    shared_freq = jnp.exp(jax.random.uniform(keys[0], (8,), jnp.float32, low, high))
    shared_phase = jax.random.uniform(keys[1], (8,), jnp.float32, -math.pi, math.pi)
    loads = jax.random.uniform(keys[2], (8, F), jnp.float32, -0.3, 0.3)
    own_freq = jnp.exp(jax.random.uniform(keys[3], (F,), jnp.float32, low, high))
    own_phase = jax.random.uniform(keys[4], (F,), jnp.float32, -math.pi, math.pi)
    offset = jax.random.uniform(keys[5], (F,), jnp.float32, -1.0, 2.0)
    own_amp = jax.random.uniform(keys[6], (F,), jnp.float32, 0.5, 1.0)
    noise = 0.25 * jnp.clip(jax.random.normal(keys[7], (FRAMES, F), jnp.float32), -3.0, 3.0)
    values = offset[None, :] + own_amp[None, :] * jnp.sin(times * own_freq[None, :] + own_phase[None, :]) + noise
    for index in range(8):
        wave = jnp.sin(times * shared_freq[index] + shared_phase[index])
        values = values + wave * loads[index][None, :]
    return values.astype(jnp.float32)


def setup_inputs(seed: int = 0) -> dict:
    key_of = jax.random.split(jax.random.key(seed), 2)
    trajectory = draw_trajectory(jax.random.fold_in(key_of[1], 71), 0)
    return {"trajectory": trajectory}


def reference(trajectory):
    frames = trajectory.shape[0]
    mean = lax.optimization_barrier(jnp.sum(trajectory, axis=0)) / frames
    centered = (trajectory - mean).astype(jnp.bfloat16)
    outs = []
    for lag in (0, 1, 4, 16):
        part = jnp.dot(centered[:frames - lag].T, centered[lag:], preferred_element_type=jnp.float32)
        outs.append(part / jnp.sqrt(jnp.float32(frames - lag)))
    return jnp.stack(outs)
```

```python
import math

import jax
import jax.numpy as jnp
from jax import lax
from jax.sharding import PartitionSpec as P

LAGS = (0, 1, 4, 16)
HALO = max(LAGS)
PAD = 16


def bits(mask):
    return [b for b in range(mask.bit_length()) if mask >> b & 1]


def last_hop(mask, half):
    return bits(mask)[-1] if half == 0 else bits(mask)[0]


def unit_order(chips):
    composite = [(m, h) for m in range(1, chips) for h in (0, 1) if len(bits(m)) > 1]
    needed = set(composite)
    for m, h in composite:
        needed.add((m ^ (1 << last_hop(m, h)), h))
    rank = lambda u: (len(bits(u[0])), u[0])
    early = sorted(needed, key=rank)
    late = [(m, h) for m in range(1, chips) for h in (1, 0) if (m, h) not in needed]
    return early + late


def tree_levels(q, count):
    def rep(low, size):
        if low <= q < low + size:
            return q
        return low + size - 1 if low + size <= q else low

    levels, size = [], 2
    while size <= count:
        moves = []
        for low in range(0, count, size):
            target = rep(low, size)
            a, b = rep(low, size // 2), rep(low + size // 2, size // 2)
            moves.append((a if target == b else b, target))
        levels.append(moves)
        size *= 2
    return levels


def shards(trajectory):
    rows, cols = trajectory.shape
    half = cols // 2
    nz, nf = lax.axis_size("tm"), lax.axis_size("feat")
    chips = nf // 2
    frames = rows * nz
    z, f = lax.axis_index("tm"), lax.axis_index("feat")
    chip, core = f // 2, f % 2
    room = 2.0 ** math.floor(math.log2(32768.0 * 1.99 / frames))

    def over_chips(value, mask):
        return lax.ppermute(value, "feat", [(i, i ^ (mask * 2)) for i in range(nf)])

    def over_core(value):
        return lax.ppermute(value, "feat", [(i, i ^ 1) for i in range(nf)])

    stats = jnp.stack([jnp.sum(trajectory, 0), jnp.max(trajectory, 0), jnp.min(trajectory, 0)])
    others = [
        lax.ppermute(stats, "tm", [(i, (i + k) % nz) for i in range(nz)]) for k in range(1, nz)
    ]
    before = lax.ppermute(trajectory[rows - HALO :], "tm", [(i, i + 1) for i in range(nz - 1)])
    total, high, low = stats
    for other in others:
        total, high, low = total + other[0], jnp.maximum(high, other[1]), jnp.minimum(low, other[2])
    mean = total / frames
    spread = jnp.max(high - low + jnp.maximum(jnp.abs(high), jnp.abs(low)) * 2.0**-14)
    power = jnp.ceil(jnp.log2(jnp.maximum(spread, 2.0**-60)))
    shrink = lax.reduce_precision(jnp.exp2(-power), 8, 7)
    grow = lax.reduce_precision(jnp.exp2(power), 8, 7)

    def centre(value):
        return ((value - mean) * shrink).astype(jnp.bfloat16)

    x = centre(trajectory)
    foot = jnp.full((PAD, half), grow, jnp.float32).astype(jnp.bfloat16)
    got = {(0, h): jnp.concatenate([x[:, h * half : (h + 1) * half], foot]) for h in (0, 1)}
    swapped = {}
    order = unit_order(chips)
    for m, h in order:
        if len(bits(m)) == 1:
            got[m, h] = over_chips(got[0, h], m)
        else:
            hop = 1 << last_hop(m, h)
            got[m, h] = over_chips(got[m ^ hop, h], hop)
    for unit in [(0, 0), (0, 1)] + order:
        swapped[unit] = over_core(got[unit])

    first = jnp.where(z == 0, jnp.bfloat16(0), centre(before))
    longer = jnp.concatenate([first, x])
    lagged = jnp.concatenate([longer[HALO - lag : HALO - lag + rows] for lag in LAGS], 1)
    lagged = lagged * jnp.bfloat16(room)

    def product(units):
        block = jnp.concatenate([part[u][:rows] for u in units for part in (got, swapped)], 1)
        return lax.dot_general(
            lagged, block, (((0,), (0,)), ((), ())), preferred_element_type=jnp.float32
        ).astype(jnp.float16)

    def summed(partial, mask):
        parts = [partial]
        for level in range(len(tree_levels(0, nz))):
            pairs = []
            for i in range(nf):
                for a, b in tree_levels(i // 2 ^ mask, nz)[level]:
                    pairs.append((a * nf + i, b * nf + i))
            sent = sum(p.astype(jnp.float32) for p in parts).astype(jnp.float16)
            parts.append(lax.ppermute(sent, ("tm", "feat"), pairs))
        return sum(p.astype(jnp.float32) for p in parts)

    mine = chip ^ z
    out = {0: 0.0, 1: 0.0}
    slots = [[(0, 0), (0, 1)]] + [order[i : i + 2] for i in range(0, len(order), 2)]
    for slot in slots:
        groups = [slot] if len({m for m, _ in slot}) == 1 else [[u] for u in slot]
        for group in groups:
            value = summed(product(group), group[0][0])
            for i, (m, h) in enumerate(group):
                part = value[:, i * cols : (i + 1) * cols]
                out[h] = jnp.where(mine == m, part, out[h])

    scales = jnp.sqrt(jnp.float32(frames) - jnp.array(LAGS, jnp.float32))
    picked = [0.0, 0.0]
    for m in range(chips):
        for i, part in enumerate((got, swapped)):
            picked[i] = jnp.where(mine == m, part[m, 0][rows, 0].astype(jnp.float32), picked[i])
    pieces = [None] * 4
    for h in (0, 1):
        value = out[h].reshape(len(LAGS), cols, cols) / scales[:, None, None]
        near = value[:, :, :half] * (picked[0] * grow / room)
        far = value[:, :, half:] * (picked[1] * grow / room)
        pieces[h] = jnp.where(core == 0, near, far)
        pieces[2 + h] = jnp.where(core == 0, far, near)
    return jnp.concatenate(pieces, 2)


def plain(trajectory):
    rows = trajectory.shape[0]
    frames = rows * lax.axis_size("tm")
    mean = lax.psum(jnp.sum(trajectory, axis=0), "tm") / frames
    centered = (trajectory - mean).astype(jnp.bfloat16)
    gathered = lax.all_gather(centered, "feat", axis=1, tiled=True)
    steps = [(i, i - 1) for i in range(1, lax.axis_size("tm"))]
    tail = lax.ppermute(gathered[:HALO], "tm", steps)
    extended = jnp.concatenate([gathered, tail], axis=0)
    blocks = [
        lax.dot_general(
            centered,
            extended[lag : lag + rows],
            (((0,), (0,)), ((), ())),
            preferred_element_type=jnp.float32,
        )
        for lag in LAGS
    ]
    summed = lax.psum_scatter(jnp.stack(blocks), "tm", scatter_dimension=2, tiled=True)
    scales = jnp.sqrt(jnp.float32(frames) - jnp.array(LAGS, jnp.float32))
    return summed / scales[:, None, None]


def solution(mesh):
    nz, nf = mesh.shape["tm"], mesh.shape["feat"]
    paired = nf == 2 * nz and nz & (nz - 1) == 0 and nz > 1
    return jax.shard_map(
        shards if paired else plain,
        mesh=mesh,
        in_specs=(P("tm", "feat"),),
        out_specs=P(None, "feat", "tm"),
        check_vma=False,
    )
```

```python
import math

import jax
import jax.numpy as jnp
from jax import lax
from jax.experimental import pallas as pl
from jax.experimental.pallas import tpu as pltpu
from jax.sharding import PartitionSpec as P


LAGS = (0, 1, 4, 16)
HALO = max(LAGS)


def bits(mask):
    return [b for b in range(mask.bit_length()) if mask >> b & 1]


def last_hop(mask, half):
    return bits(mask)[-1] if half == 0 else bits(mask)[0]


def arrivals(chips):
    singles = [m for m in range(1, chips) if len(bits(m)) == 1]
    order = [(m, i % 2) for i, m in enumerate(singles)]
    order += [(m, 1 - i % 2) for i, m in enumerate(singles)]
    if len(singles) % 2:
        order = [(m, h) for m in singles for h in (0, 1)]
    several = [m for m in range(1, chips) if len(bits(m)) > 1]
    order += [(m, h) for m in sorted(several, key=lambda m: len(bits(m))) for h in (0, 1)]
    return [order[i : i + 2] for i in range(0, len(order), 2)]


def tree_levels(q, count):
    def rep(low, size):
        if low <= q < low + size:
            return q
        return low + size - 1 if low + size <= q else low

    levels, size = [], 2
    while size <= count:
        moves = []
        for low in range(0, count, size):
            target = rep(low, size)
            a, b = rep(low, size // 2), rep(low + size // 2, size // 2)
            moves.append((a if target == b else b, target))
        levels.append(moves)
        size *= 2
    return levels


def lagged_kernel(own_ref, own_next_ref, other_ref, other_next_ref, out_ref, wide_ref, exact_ref):
    rows, cols = own_ref.shape
    for i, (ref, after) in enumerate(((own_ref, own_next_ref), (other_ref, other_next_ref))):
        exact_ref[:rows] = ref[...]
        exact_ref[rows:] = after[...]
        wide_ref[:rows] = ref[...].astype(jnp.float32)
        wide_ref[rows:] = after[...].astype(jnp.float32)
        for k, lag in enumerate(LAGS):
            start = HALO - lag
            source = exact_ref if start % 16 == 0 else wide_ref
            at = (len(LAGS) * i + k) * cols
            out_ref[:, at : at + cols] = source[start : start + rows].astype(out_ref.dtype)


def lagged_columns(own, other):
    rows, cols = own.shape[0] - HALO, own.shape[1]
    step = math.gcd(rows, 512)
    main = pl.BlockSpec((step, cols), lambda i: (i, 0))
    after = pl.BlockSpec((HALO, cols), lambda i: ((i + 1) * (step // HALO), 0))
    wide = 2 * len(LAGS) * cols

    def body(own_ref, own_next_ref, other_ref, other_next_ref, out_ref, wide_ref, exact_ref):
        rows_here = pl.ds(pl.multiple_of(pl.program_id(0) * step, step), step)
        lagged_kernel(
            own_ref, own_next_ref, other_ref, other_next_ref, out_ref.at[rows_here], wide_ref, exact_ref
        )

    return pl.pallas_call(
        body,
        out_shape=pltpu.VMEM((rows, wide), own.dtype),
        grid=(rows // step,),
        in_specs=[main, after, main, after],
        out_specs=pl.BlockSpec(memory_space=pltpu.VMEM),
        scratch_shapes=[
            pltpu.VMEM((step + HALO, cols), jnp.float32),
            pltpu.VMEM((step + HALO, cols), own.dtype),
        ],
        cost_estimate=pl.CostEstimate(
            flops=rows * wide, bytes_accessed=2 * rows * (wide + 2 * cols), transcendentals=0
        ),
        compiler_params=pltpu.CompilerParams(vmem_limit_bytes=16 * 1024 * 1024),
        name="lagged",
    )(own, own, other, other)


def make(mesh):
    nz, nf = mesh.shape["tm"], mesh.shape["feat"]
    chips = nf // 2
    levels = nz.bit_length() - 1

    def shards(trajectory):
        rows, cols = trajectory.shape
        half = cols // 2
        tall = len(LAGS) * cols
        frames = rows * nz
        z, f = lax.axis_index("tm"), lax.axis_index("feat")
        chip, core = lax.div(f, 2), lax.rem(f, 2)
        mine = lax.bitwise_xor(chip, z)
        room = 2.0 ** math.floor(math.log2(32768.0 / frames))

        def hop(mask):
            return [(i, i ^ mask) for i in range(nf)]

        stats = jnp.stack([jnp.sum(trajectory, 0), jnp.max(trajectory, 0), jnp.min(trajectory, 0)])
        others = [
            lax.ppermute(stats, "tm", [(i, (i + k) % nz) for i in range(nz)])
            for k in range(1, nz)
        ]
        total, high, low = stats
        for other in others:
            total = total + other[0]
            high, low = jnp.maximum(high, other[1]), jnp.minimum(low, other[2])
        mean = total / frames
        spread = high - low + jnp.maximum(jnp.abs(high), jnp.abs(low)) * 2.0**-14
        power = jnp.ceil(jnp.log2(jnp.maximum(spread, 2.0**-60)))
        shrink = lax.reduce_precision(jnp.exp2(-power), 8, 7)
        grow = lax.reduce_precision(jnp.exp2(power), 8, 7)

        def centre(value, low=0, high=cols):
            return ((value - mean[low:high]) * shrink[low:high]).astype(jnp.bfloat16)

        got = {}
        for h in (0, 1):
            low, high = h * half, (h + 1) * half
            got[0, h] = centre(trajectory[:, low:high], low, high)
            mean, shrink, got[0, h] = lax.optimization_barrier((mean, shrink, got[0, h]))
        slots = arrivals(chips)
        for slot in slots:
            for m, h in slot:
                if len(bits(m)) == 1:
                    got[m, h] = lax.ppermute(got[0, h], "feat", hop(2 * m))

        before = lax.ppermute(trajectory[rows - HALO :], "tm", [(i, i + 1) for i in range(nz - 1)])
        first = jnp.where(z == 0, jnp.bfloat16(0), centre(before))
        own = jnp.concatenate([first, jnp.concatenate([got[0, 0], got[0, 1]], 1)])
        lagged = lagged_columns(own, lax.ppermute(own, "feat", hop(1)))

        turned = lax.ppermute(grow[None], "feat", hop(1))[0]
        pair = jnp.stack([jnp.where(core == 0, grow, turned), jnp.where(core == 0, turned, grow)])
        across = pair
        for m in range(1, chips):
            across = jnp.where(mine == m, lax.ppermute(pair, "feat", hop(2 * m)), across)

        def product(blocks, low=0, high=2 * tall):
            value = lax.dot_general(
                lagged[:, low:high],
                jnp.concatenate(blocks, 1) if len(blocks) > 1 else blocks[0],
                (((0,), (0,)), ((), ())),
                preferred_element_type=jnp.float32,
            )
            return (value * room).astype(jnp.float16)

        def wide(value):
            return value.astype(jnp.float32)

        def rise(mask, level, flip=0):
            return [
                (x * nf + j, y * nf + (j ^ flip))
                for j in range(nf)
                for x, y in tree_levels(j // 2 ^ mask, nz)[level]
            ]

        both = ("tm", "feat")
        top = levels - 1
        none = jnp.float32(0)

        def add(values):
            total = wide(values[0])
            for value in values[1:]:
                total = total + wide(value)
            return total

        def climbed(part, mask, until):
            terms = [part]
            for level in range(until):
                sent = part if level == 0 else add(terms).astype(jnp.float16)
                terms.append(lax.ppermute(sent, both, rise(mask, level)))
            return terms

        part = product([own[HALO:]])
        terms = climbed(part, 0, top)
        terms.append(lax.ppermute(add(terms).astype(jnp.float16), both, rise(0, top)))
        kept = [[(0, [v[:, h * half : (h + 1) * half] for v in terms])] for h in (0, 1)]

        for slot in slots:
            for m, h in slot:
                if len(bits(m)) > 1:
                    axis = 1 << last_hop(m, h)
                    got[m, h] = lax.ppermute(got[m ^ axis, h], "feat", hop(2 * axis))

        late = [[], []]
        for s, slot in enumerate(slots):
            (a, ha), (b, hb) = slot
            blocks = [got[u] for u in slot]
            if a != b:
                if s == 0:
                    part = product(blocks)
                else:
                    part = jnp.concatenate(
                        [product(blocks, i * tall, (i + 1) * tall) for i in (0, 1)]
                    )
                sides = [
                    climbed(part[:, i * half : (i + 1) * half], m, top)
                    for i, (m, _) in enumerate(slot)
                ]
                pairs = rise(a, top) + rise(b, top)
                assert all(len({p[i] for p in pairs}) == len(pairs) for i in (0, 1))
                sender = sum(
                    jnp.where(lax.bitwise_xor(chip, a) == q, tree_levels(q, nz)[top][0][0], 0)
                    for q in range(nz)
                )
                sent = jnp.where(z == sender, *map(add, sides)).astype(jnp.float16)
                back = lax.ppermute(sent, both, pairs)
                kept[ha].append((a, sides[0] + [back]))
                kept[hb].append((b, sides[1] + [back]))
                continue
            sums = []
            for i in (0, 1):
                part = product(blocks, i * tall, (i + 1) * tall)
                terms = climbed(part, a, top)
                sent = add(terms).astype(jnp.float16)
                late[i].append(lax.ppermute(sent, both, rise(a, top, i)))
                sums.append(terms)
            kept[ha].append((a, [[v[:, :half] for v in terms] for terms in sums]))
            kept[hb].append((b, [[v[:, half:] for v in terms] for terms in sums]))

        sides = []
        for i in (0, 1):
            columns = []
            for h in (0, 1):
                total = none
                for m, terms in kept[h]:
                    if isinstance(terms[0], list):
                        terms = terms[i]
                    else:
                        terms = [v[i * tall : (i + 1) * tall] for v in terms]
                    total = jnp.where(mine == m, add(terms), total)
                columns.append(total)
            sides.append(jnp.concatenate(columns, 1))
        near, theirs = sides[0], lax.ppermute(sides[1], "feat", hop(1))

        scales = 1 / (jnp.sqrt(jnp.float32(frames) - jnp.array(LAGS, jnp.float32)) * room)
        out = jnp.zeros((len(LAGS), cols, 2 * cols), jnp.float32)
        for value, added, owner in ((near, late[0], core), (theirs, late[1], 1 - core)):
            for more in added:
                value = value + wide(more)
            value = value.reshape(len(LAGS), cols, cols) * scales[:, None, None]
            value = value * grow[None, :, None] * jnp.where(owner == 0, across[0], across[1])
            out = lax.dynamic_update_slice(out, value, (0, 0, owner * cols))
        return out

    return shards


def plain(trajectory):
    rows = trajectory.shape[0]
    frames = rows * lax.axis_size("tm")
    mean = lax.psum(jnp.sum(trajectory, axis=0), "tm") / frames
    centered = (trajectory - mean).astype(jnp.bfloat16)
    gathered = lax.all_gather(centered, "feat", axis=1, tiled=True)
    steps = [(i, i - 1) for i in range(1, lax.axis_size("tm"))]
    tail = lax.ppermute(gathered[:HALO], "tm", steps)
    extended = jnp.concatenate([gathered, tail], axis=0)
    blocks = [
        lax.dot_general(
            centered,
            extended[lag : lag + rows],
            (((0,), (0,)), ((), ())),
            preferred_element_type=jnp.float32,
        )
        for lag in LAGS
    ]
    summed = lax.psum_scatter(jnp.stack(blocks), "tm", scatter_dimension=2, tiled=True)
    scales = jnp.sqrt(jnp.float32(frames) - jnp.array(LAGS, jnp.float32))
    return summed / scales[:, None, None]


def solution(mesh):
    nz, nf = mesh.shape["tm"], mesh.shape["feat"]
    paired = nf == 2 * nz and nz & (nz - 1) == 0 and nz > 2
    body = make(mesh) if paired else plain

    return jax.shard_map(
        body,
        mesh=mesh,
        in_specs=(P("tm", "feat"),),
        out_specs=P(None, "feat", "tm"),
        check_vma=False,
    )
```

```python
import math

import jax
import jax.numpy as jnp
from jax import lax
from jax.experimental import pallas as pl
from jax.experimental.pallas import tpu as pltpu
from jax.sharding import PartitionSpec as P


LAGS = (0, 1, 4, 16)
HALO = max(LAGS)


def bits(mask):
    return [b for b in range(mask.bit_length()) if mask >> b & 1]


def last_hop(mask, half):
    return bits(mask)[-1] if half == 0 else bits(mask)[0]


def arrivals(chips):
    singles = [m for m in range(1, chips) if len(bits(m)) == 1]
    order = [(m, i % 2) for i, m in enumerate(singles)]
    order += [(m, 1 - i % 2) for i, m in enumerate(singles)]
    if len(singles) % 2:
        order = [(m, h) for m in singles for h in (0, 1)]
    several = [m for m in range(1, chips) if len(bits(m)) > 1]
    order += [(m, h) for m in sorted(several, key=lambda m: len(bits(m))) for h in (0, 1)]
    return [order[i : i + 2] for i in range(0, len(order), 2)]


def tree_levels(q, count):
    def rep(low, size):
        if low <= q < low + size:
            return q
        return low + size - 1 if low + size <= q else low

    levels, size = [], 2
    while size <= count:
        moves = []
        for low in range(0, count, size):
            target = rep(low, size)
            a, b = rep(low, size // 2), rep(low + size // 2, size // 2)
            moves.append((a if target == b else b, target))
        levels.append(moves)
        size *= 2
    return levels


def lagged_kernel(*refs):
    out_ref, wide_ref, exact_ref = refs[-3:]
    rows, cols = wide_ref.shape[0] - HALO, wide_ref.shape[1]
    half = cols // 2
    step = pl.program_id(0)
    here = pl.ds(pl.multiple_of(step * rows, rows), rows)
    for i in (0, 1):
        first_ref, *parts = refs[5 * i : 5 * i + 5]
        for h in (0, 1):
            main_ref, prior_ref = parts[2 * h : 2 * h + 2]
            columns = slice(h * half, (h + 1) * half)
            prior = jnp.where(step == 0, first_ref[:, columns], prior_ref[...])
            exact_ref[:HALO, columns] = prior
            exact_ref[HALO:, columns] = main_ref[...]
            wide_ref[:HALO, columns] = prior.astype(jnp.float32)
            wide_ref[HALO:, columns] = main_ref[...].astype(jnp.float32)
        for k, lag in enumerate(LAGS):
            start = HALO - lag
            source = exact_ref if start % 16 == 0 else wide_ref
            at = (len(LAGS) * i + k) * cols
            out_ref[here, at : at + cols] = source[start : start + rows].astype(out_ref.dtype)


def lagged_columns(own, other):
    rows, half = own[1].shape
    cols = 2 * half
    step = math.gcd(rows, 512)
    wide = 2 * len(LAGS) * cols
    first = pl.BlockSpec((HALO, cols), lambda i: (0, 0))
    main = pl.BlockSpec((step, half), lambda i: (i, 0))
    prior = pl.BlockSpec((HALO, half), lambda i: (jnp.maximum(i * (step // HALO) - 1, 0), 0))
    operands = [v for before, a, b in (own, other) for v in (before, a, a, b, b)]
    return pl.pallas_call(
        lagged_kernel,
        out_shape=pltpu.VMEM((rows, wide), own[1].dtype),
        grid=(rows // step,),
        in_specs=[first, main, prior, main, prior] * 2,
        out_specs=pl.BlockSpec(memory_space=pltpu.VMEM),
        scratch_shapes=[
            pltpu.VMEM((step + HALO, cols), jnp.float32),
            pltpu.VMEM((step + HALO, cols), own[1].dtype),
        ],
        cost_estimate=pl.CostEstimate(
            flops=rows * wide, bytes_accessed=2 * rows * (wide + 2 * cols), transcendentals=0
        ),
        compiler_params=pltpu.CompilerParams(vmem_limit_bytes=16 * 1024 * 1024),
        name="lagged",
    )(*operands)


def join_kernel(left_ref, right_ref, out_ref, sems):
    cols = left_ref.shape[1]
    copies = [
        pltpu.make_async_copy(ref, out_ref.at[:, i * cols : (i + 1) * cols], sems.at[i])
        for i, ref in enumerate((left_ref, right_ref))
    ]
    for copy in copies:
        copy.start()
    for copy in copies:
        copy.wait()


def joined(left, right):
    rows, cols = left.shape
    anywhere = pl.BlockSpec(memory_space=pl.ANY)
    if cols % 128:
        return jnp.concatenate([left, right], 1)
    return pl.pallas_call(
        join_kernel,
        out_shape=pltpu.VMEM((rows, 2 * cols), left.dtype),
        in_specs=[anywhere, anywhere],
        out_specs=pl.BlockSpec(memory_space=pltpu.VMEM),
        scratch_shapes=[pltpu.SemaphoreType.DMA((2,))],
        cost_estimate=pl.CostEstimate(flops=0, bytes_accessed=8 * rows * cols, transcendentals=0),
        compiler_params=pltpu.CompilerParams(vmem_limit_bytes=1024 * 1024),
        name="join",
    )(left, right)


def make(mesh):
    nz, nf = mesh.shape["tm"], mesh.shape["feat"]
    chips = nf // 2
    levels = nz.bit_length() - 1

    def shards(trajectory):
        rows, cols = trajectory.shape
        half = cols // 2
        tall = len(LAGS) * cols
        frames = rows * nz
        z, f = lax.axis_index("tm"), lax.axis_index("feat")
        chip, core = lax.div(f, 2), lax.rem(f, 2)
        mine = lax.bitwise_xor(chip, z)
        room = 2.0 ** math.floor(math.log2(32768.0 / frames))

        def hop(mask):
            return [(i, i ^ mask) for i in range(nf)]

        stats = jnp.stack([jnp.sum(trajectory, 0), jnp.max(trajectory, 0), jnp.min(trajectory, 0)])
        others = [
            lax.ppermute(stats, "tm", [(i, (i + k) % nz) for i in range(nz)])
            for k in range(1, nz)
        ]
        total, high, low = stats
        for other in others:
            total = total + other[0]
            high, low = jnp.maximum(high, other[1]), jnp.minimum(low, other[2])
        mean = total / frames
        spread = high - low + jnp.maximum(jnp.abs(high), jnp.abs(low)) * 2.0**-14
        power = jnp.ceil(jnp.log2(jnp.maximum(spread, 2.0**-60)))
        shrink = lax.reduce_precision(jnp.exp2(-power), 8, 7)
        grow = lax.reduce_precision(jnp.exp2(power), 8, 7)

        def centre(value, low=0, high=cols):
            return ((value - mean[low:high]) * shrink[low:high]).astype(jnp.bfloat16)

        got = {}
        for h in (0, 1):
            low, high = h * half, (h + 1) * half
            got[0, h] = centre(trajectory[:, low:high], low, high)
            mean, shrink, got[0, h] = lax.optimization_barrier((mean, shrink, got[0, h]))
        slots = arrivals(chips)
        for slot in slots:
            for m, h in slot:
                if len(bits(m)) == 1:
                    got[m, h] = lax.ppermute(got[0, h], "feat", hop(2 * m))

        swapped = [lax.ppermute(got[0, h], "feat", hop(1)) for h in (0, 1)]
        tail, got[0, 1] = lax.optimization_barrier((trajectory, got[0, 1]))
        before = lax.ppermute(tail[rows - HALO :], "tm", [(i, i + 1) for i in range(nz - 1)])
        first = jnp.where(z == 0, jnp.bfloat16(0), centre(before))
        lagged = lagged_columns(
            (first, got[0, 0], got[0, 1]), (lax.ppermute(first, "feat", hop(1)), *swapped)
        )

        turned = lax.ppermute(grow[None], "feat", hop(1))[0]
        pair = jnp.stack([jnp.where(core == 0, grow, turned), jnp.where(core == 0, turned, grow)])
        across = pair
        for m in range(1, chips):
            across = jnp.where(mine == m, lax.ppermute(pair, "feat", hop(2 * m)), across)

        def product(block, low=0, high=2 * tall):
            value = lax.dot_general(
                block,
                lagged[:, low:high],
                (((0,), (0,)), ((), ())),
                preferred_element_type=jnp.float32,
            )
            return (value * room).astype(jnp.float16)

        def wide(value):
            return value.astype(jnp.float32)

        def rise(mask, level, flip=0):
            return [
                (x * nf + j, y * nf + (j ^ flip))
                for j in range(nf)
                for x, y in tree_levels(j // 2 ^ mask, nz)[level]
            ]

        both = ("tm", "feat")
        top = levels - 1
        none = jnp.float32(0)

        def add(values):
            total = wide(values[0])
            for value in values[1:]:
                total = total + wide(value)
            return total

        def climbed(part, mask, until):
            terms = [part]
            for level in range(until):
                sent = part if level == 0 else add(terms).astype(jnp.float16)
                terms.append(lax.ppermute(sent, both, rise(mask, level)))
            return terms

        part = product(joined(got[0, 0], got[0, 1]))
        terms = climbed(part, 0, top)
        terms.append(lax.ppermute(add(terms).astype(jnp.float16), both, rise(0, top)))
        kept = [[(0, [v[h * half : (h + 1) * half] for v in terms])] for h in (0, 1)]

        for slot in slots:
            for m, h in slot:
                if len(bits(m)) > 1:
                    axis = 1 << last_hop(m, h)
                    got[m, h] = lax.ppermute(got[m ^ axis, h], "feat", hop(2 * axis))

        late = [[], []]
        for slot in slots:
            (a, ha), (b, hb) = slot
            block = joined(*[got[u] for u in slot])
            if a != b:
                part = product(block)
                sides = [part[:half], part[half:]]
                terms = [jnp.where(mine == a, *sides)]
                for k in range(1, nz):
                    pairs = [
                        (y * nf + i, (y ^ k) * nf + i)
                        for i in range(nf)
                        for y in range(nz)
                        if i // 2 ^ y ^ k in (a, b)
                    ]
                    sent = jnp.where(lax.bitwise_xor(mine, k) == a, *sides)
                    terms.append(lax.ppermute(sent, both, pairs))
                kept[ha].append((a, terms))
                kept[hb].append((b, terms))
                continue
            sums = []
            for i in (0, 1):
                part = product(block, i * tall, (i + 1) * tall)
                terms = climbed(part, a, top)
                sent = add(terms).astype(jnp.float16)
                late[i].append(lax.ppermute(sent, both, rise(a, top, i)))
                sums.append(terms)
            kept[ha].append((a, [[v[:half] for v in terms] for terms in sums]))
            kept[hb].append((b, [[v[half:] for v in terms] for terms in sums]))

        def owned(m):
            terms = [dict(kept[h])[m] for h in (0, 1)]

            def branch(both_terms):
                sides = []
                for i in (0, 1):
                    columns = []
                    for values in both_terms:
                        if isinstance(values[0], list):
                            values = values[i]
                        else:
                            values = [v[:, i * tall : (i + 1) * tall] for v in values]
                        columns.append(add(values))
                    sides.append(jnp.concatenate(columns))
                return sides

            return lambda: branch(terms)

        sides = lax.switch(mine, [owned(m) for m in range(chips)])
        near, theirs = sides[0], lax.ppermute(sides[1], "feat", hop(1))
        scales = 1 / (jnp.sqrt(jnp.float32(frames) - jnp.array(LAGS, jnp.float32)) * room)
        out = jnp.zeros((len(LAGS), cols, 2 * cols), jnp.float32)
        for value, added, owner in ((near, late[0], core), (theirs, late[1], 1 - core)):
            for more in added:
                value = value + wide(more)
            value = value.T.reshape(len(LAGS), cols, cols) * scales[:, None, None]
            value = value * grow[None, :, None] * jnp.where(owner == 0, across[0], across[1])
            out = lax.dynamic_update_slice(out, value, (0, 0, owner * cols))
        return out

    return shards


def plain(trajectory):
    rows = trajectory.shape[0]
    frames = rows * lax.axis_size("tm")
    mean = lax.psum(jnp.sum(trajectory, axis=0), "tm") / frames
    centered = (trajectory - mean).astype(jnp.bfloat16)
    gathered = lax.all_gather(centered, "feat", axis=1, tiled=True)
    steps = [(i, i - 1) for i in range(1, lax.axis_size("tm"))]
    tail = lax.ppermute(gathered[:HALO], "tm", steps)
    extended = jnp.concatenate([gathered, tail], axis=0)
    blocks = [
        lax.dot_general(
            centered,
            extended[lag : lag + rows],
            (((0,), (0,)), ((), ())),
            preferred_element_type=jnp.float32,
        )
        for lag in LAGS
    ]
    summed = lax.psum_scatter(jnp.stack(blocks), "tm", scatter_dimension=2, tiled=True)
    scales = jnp.sqrt(jnp.float32(frames) - jnp.array(LAGS, jnp.float32))
    return summed / scales[:, None, None]


def solution(mesh):
    nz, nf = mesh.shape["tm"], mesh.shape["feat"]
    paired = nf == 2 * nz and nz & (nz - 1) == 0 and nz > 2
    body = make(mesh) if paired else plain

    return jax.shard_map(
        body,
        mesh=mesh,
        in_specs=(P("tm", "feat"),),
        out_specs=P(None, "feat", "tm"),
        check_vma=False,
    )
```

```python
import math

import jax
import jax.numpy as jnp
from jax import lax
from jax.experimental import pallas as pl
from jax.experimental.pallas import tpu as pltpu
from jax.sharding import PartitionSpec as P


LAGS = (0, 1, 4, 16)
HALO = max(LAGS)


def bits(mask):
    return [b for b in range(mask.bit_length()) if mask >> b & 1]


def last_hop(mask, half):
    return bits(mask)[-1] if half == 0 else bits(mask)[0]


def arrivals(chips):
    singles = [m for m in range(1, chips) if len(bits(m)) == 1]
    order = [(m, i % 2) for i, m in enumerate(singles)]
    order += [(m, 1 - i % 2) for i, m in enumerate(singles)]
    if len(singles) % 2:
        order = [(m, h) for m in singles for h in (0, 1)]
    several = [m for m in range(1, chips) if len(bits(m)) > 1]
    order += [(m, h) for m in sorted(several, key=lambda m: len(bits(m))) for h in (0, 1)]
    return [order[i : i + 2] for i in range(0, len(order), 2)]


def tree_levels(q, count):
    def rep(low, size):
        if low <= q < low + size:
            return q
        return low + size - 1 if low + size <= q else low

    levels, size = [], 2
    while size <= count:
        moves = []
        for low in range(0, count, size):
            target = rep(low, size)
            a, b = rep(low, size // 2), rep(low + size // 2, size // 2)
            moves.append((a if target == b else b, target))
        levels.append(moves)
        size *= 2
    return levels


def chain_levels(q, count):
    return [
        [(k, k + 1)] * (k < q) + [(count - 1 - k, count - 2 - k)] * (count - 1 - k > q)
        for k in range(count - 1)
    ]


def lagged_kernel(*refs):
    out_ref, wide_ref, exact_ref = refs[-3:]
    rows, cols = wide_ref.shape[0] - HALO, wide_ref.shape[1]
    half = cols // 2
    step = pl.program_id(0)
    here = pl.ds(pl.multiple_of(step * rows, rows), rows)
    for i in (0, 1):
        first_ref, *parts = refs[5 * i : 5 * i + 5]
        for h in (0, 1):
            main_ref, prior_ref = parts[2 * h : 2 * h + 2]
            columns = slice(h * half, (h + 1) * half)
            prior = jnp.where(step == 0, first_ref[:, columns], prior_ref[...])
            exact_ref[:HALO, columns] = prior
            exact_ref[HALO:, columns] = main_ref[...]
            wide_ref[:HALO, columns] = prior.astype(jnp.float32)
            wide_ref[HALO:, columns] = main_ref[...].astype(jnp.float32)
        for k, lag in enumerate(LAGS):
            start = HALO - lag
            source = exact_ref if start % 16 == 0 else wide_ref
            at = (len(LAGS) * i + k) * cols
            out_ref[here, at : at + cols] = source[start : start + rows].astype(out_ref.dtype)


def lagged_columns(own, other):
    rows, half = own[1].shape
    cols = 2 * half
    step = math.gcd(rows, 512)
    wide = 2 * len(LAGS) * cols
    first = pl.BlockSpec((HALO, cols), lambda i: (0, 0))
    main = pl.BlockSpec((step, half), lambda i: (i, 0))
    prior = pl.BlockSpec((HALO, half), lambda i: (jnp.maximum(i * (step // HALO) - 1, 0), 0))
    operands = [v for before, a, b in (own, other) for v in (before, a, a, b, b)]
    return pl.pallas_call(
        lagged_kernel,
        out_shape=pltpu.VMEM((rows, wide), own[1].dtype),
        grid=(rows // step,),
        in_specs=[first, main, prior, main, prior] * 2,
        out_specs=pl.BlockSpec(memory_space=pltpu.VMEM),
        scratch_shapes=[
            pltpu.VMEM((step + HALO, cols), jnp.float32),
            pltpu.VMEM((step + HALO, cols), own[1].dtype),
        ],
        cost_estimate=pl.CostEstimate(
            flops=rows * wide, bytes_accessed=2 * rows * (wide + 2 * cols), transcendentals=0
        ),
        compiler_params=pltpu.CompilerParams(vmem_limit_bytes=16 * 1024 * 1024),
        name="lagged",
    )(*operands)


def join_kernel(left_ref, right_ref, out_ref, sems):
    cols = left_ref.shape[1]
    copies = [
        pltpu.make_async_copy(ref, out_ref.at[:, i * cols : (i + 1) * cols], sems.at[i])
        for i, ref in enumerate((left_ref, right_ref))
    ]
    for copy in copies:
        copy.start()
    for copy in copies:
        copy.wait()


def joined(left, right):
    rows, cols = left.shape
    anywhere = pl.BlockSpec(memory_space=pl.ANY)
    if cols % 128:
        return jnp.concatenate([left, right], 1)
    return pl.pallas_call(
        join_kernel,
        out_shape=pltpu.VMEM((rows, 2 * cols), left.dtype),
        in_specs=[anywhere, anywhere],
        out_specs=pl.BlockSpec(memory_space=pltpu.VMEM),
        scratch_shapes=[pltpu.SemaphoreType.DMA((2,))],
        cost_estimate=pl.CostEstimate(flops=0, bytes_accessed=8 * rows * cols, transcendentals=0),
        compiler_params=pltpu.CompilerParams(vmem_limit_bytes=1024 * 1024),
        name="join",
    )(left, right)


def order_kernel(flag_ref, a_ref, b_ref, lead_ref, rest_ref, sems):
    def copied(lead, rest):
        copies = [
            pltpu.make_async_copy(lead, lead_ref, sems.at[0]),
            pltpu.make_async_copy(rest, rest_ref, sems.at[1]),
        ]
        for copy in copies:
            copy.start()
        for copy in copies:
            copy.wait()

    @pl.when(flag_ref[0] == 1)
    def _():
        copied(a_ref, b_ref)

    @pl.when(flag_ref[0] != 1)
    def _():
        copied(b_ref, a_ref)


def ordered(flag, a, b):
    anywhere = pl.BlockSpec(memory_space=pl.ANY)
    return pl.pallas_call(
        order_kernel,
        out_shape=[pltpu.VMEM(a.shape, a.dtype)] * 2,
        in_specs=[pl.BlockSpec(memory_space=pltpu.SMEM), anywhere, anywhere],
        out_specs=[pl.BlockSpec(memory_space=pltpu.VMEM)] * 2,
        scratch_shapes=[pltpu.SemaphoreType.DMA((2,))],
        cost_estimate=pl.CostEstimate(
            flops=0, bytes_accessed=8 * a.shape[0] * a.shape[1], transcendentals=0
        ),
        compiler_params=pltpu.CompilerParams(vmem_limit_bytes=1024 * 1024),
        name="order",
    )(flag.astype(jnp.int32)[None], a, b)


def finish_kernel(core_ref, rows_ref, across_ref, *refs):
    out_ref = refs[-1]
    half = refs[0].shape[0]
    for i in (0, 1):
        owner = core_ref[0] if i == 0 else 1 - core_ref[0]
        for h in (0, 1):
            at = pl.ds(pl.multiple_of((2 * owner + h) * half, half), half)
            tall = rows_ref.shape[2]
            here = pl.ds(pl.multiple_of(pl.program_id(0) * tall, tall), tall)
            value = (refs[2 * i + h][:, here] * rows_ref[0]).T
            out_ref[0, :, at] = value * across_ref[:, at]


def finished(core, rows, across, pieces):
    lags, _, tall = rows.shape
    half = pieces[0].shape[0]
    wide = 4 * half
    if half % 128:
        order = lambda i: [jnp.where(core == i, pieces[h], pieces[2 + h]) for h in (0, 1)]
        value = jnp.concatenate(order(0) + order(1)).T.reshape(lags, tall, wide)
        return value * rows.transpose(0, 2, 1) * across
    return pl.pallas_call(
        finish_kernel,
        out_shape=jax.ShapeDtypeStruct((lags, tall, wide), jnp.float32),
        grid=(lags,),
        in_specs=[
            pl.BlockSpec(memory_space=pltpu.SMEM),
            pl.BlockSpec((1, 1, tall), lambda k: (k, 0, 0)),
            pl.BlockSpec((1, wide), lambda k: (0, 0)),
        ]
        + [pl.BlockSpec(memory_space=pltpu.VMEM)] * 4,
        out_specs=pl.BlockSpec((1, tall, wide), lambda k: (k, 0, 0)),
        cost_estimate=pl.CostEstimate(
            flops=2 * lags * tall * wide, bytes_accessed=8 * lags * tall * wide, transcendentals=0
        ),
        compiler_params=pltpu.CompilerParams(vmem_limit_bytes=16 * 1024 * 1024),
        name="finish",
    )(core[None], rows, across, *pieces)


def make(mesh):
    nz, nf = mesh.shape["tm"], mesh.shape["feat"]
    chips = nf // 2
    levels = nz.bit_length() - 1

    def shards(trajectory):
        rows, cols = trajectory.shape
        half = cols // 2
        tall = len(LAGS) * cols
        frames = rows * nz
        z, f = lax.axis_index("tm"), lax.axis_index("feat")
        chip, core = lax.div(f, 2), lax.rem(f, 2)
        mine = lax.bitwise_xor(chip, z)
        room = 2.0 ** math.floor(math.log2(32768.0 / frames))

        def hop(mask):
            return [(i, i ^ mask) for i in range(nf)]

        stats = jnp.stack([jnp.sum(trajectory, 0), jnp.max(trajectory, 0), jnp.min(trajectory, 0)])
        others = [
            lax.ppermute(stats, "tm", [(i, i ^ k) for i in range(nz)])
            for k in reversed(range(1, nz))
        ]
        total, high, low = stats
        for other in others:
            total = total + other[0]
            high, low = jnp.maximum(high, other[1]), jnp.minimum(low, other[2])
        mean = total / frames
        spread = high - low + jnp.maximum(jnp.abs(high), jnp.abs(low)) * 2.0**-14
        power = jnp.ceil(jnp.log2(jnp.maximum(spread, 2.0**-60)))
        shrink = lax.reduce_precision(jnp.exp2(-power), 8, 7)
        grow = lax.reduce_precision(jnp.exp2(power), 8, 7)

        def centre(value, low=0, high=cols):
            return ((value - mean[low:high]) * shrink[low:high]).astype(jnp.bfloat16)

        got = {}
        for h in (0, 1):
            low, high = h * half, (h + 1) * half
            got[0, h] = centre(trajectory[:, low:high], low, high)
            mean, shrink, got[0, h] = lax.optimization_barrier((mean, shrink, got[0, h]))
        slots = arrivals(chips)
        for slot in slots:
            for m, h in slot:
                if len(bits(m)) == 1:
                    got[m, h] = lax.ppermute(got[0, h], "feat", hop(2 * m))

        swapped = [lax.ppermute(got[0, h], "feat", hop(1)) for h in (0, 1)]
        tail, got[0, 1] = lax.optimization_barrier((trajectory, got[0, 1]))
        before = lax.ppermute(tail[rows - HALO :], "tm", [(i, i + 1) for i in range(nz - 1)])
        first = jnp.where(z == 0, jnp.bfloat16(0), centre(before))
        lagged = lagged_columns(
            (first, got[0, 0], got[0, 1]), (lax.ppermute(first, "feat", hop(1)), *swapped)
        )

        turned = lax.ppermute(grow[None], "feat", hop(1))[0]
        pair = jnp.stack([jnp.where(core == 0, grow, turned), jnp.where(core == 0, turned, grow)])
        across = pair
        for m in range(1, chips):
            across = jnp.where(mine == m, lax.ppermute(pair, "feat", hop(2 * m)), across)

        def product(block, low=0, high=2 * tall):
            value = lax.dot_general(
                block,
                lagged[:, low:high],
                (((0,), (0,)), ((), ())),
                preferred_element_type=jnp.float32,
            )
            return (value * room).astype(jnp.float16)

        def wide(value):
            return value.astype(jnp.float32)

        def rise(mask, level, flip=0, plan=tree_levels):
            return [
                (x * nf + j, y * nf + (j ^ flip))
                for j in range(nf)
                for x, y in plan(j // 2 ^ mask, nz)[level]
            ]

        both = ("tm", "feat")
        top = levels - 1
        none = jnp.float32(0)

        def add(values):
            total = wide(values[0])
            for value in values[1:]:
                total = total + wide(value)
            return total

        def climbed(part, mask, until, plan=tree_levels):
            terms = [part]
            for level in range(until):
                sent = part if level == 0 else add(terms).astype(jnp.float16)
                terms.append(lax.ppermute(sent, both, rise(mask, level, 0, plan)))
            return terms

        part = product(joined(got[0, 0], got[0, 1]))
        terms = climbed(part, 0, top)
        terms.append(lax.ppermute(add(terms).astype(jnp.float16), both, rise(0, top)))
        kept = [[(0, [v[h * half : (h + 1) * half] for v in terms])] for h in (0, 1)]

        for slot in slots:
            for m, h in slot:
                if len(bits(m)) > 1:
                    axis = 1 << last_hop(m, h)
                    got[m, h] = lax.ppermute(got[m ^ axis, h], "feat", hop(2 * axis))

        late = [[[], []], [[], []]]
        for slot in slots:
            (a, ha), (b, hb) = slot
            if a != b:
                low = (a ^ b) & -(a ^ b)
                flag = lax.bitwise_and(lax.bitwise_xor(mine, a), low) != 0
                blocks = ordered(flag, got[a, ha], got[b, hb])
                back = {}
                for leading, block in ((True, blocks[0]), (False, blocks[1])):
                    part = product(block)
                    for k in range(1, nz):
                        if bool(k & low) == leading:
                            pairs = [
                                (y * nf + i, (y ^ k) * nf + i)
                                for i in range(nf)
                                for y in range(nz)
                                if i // 2 ^ y ^ k in (a, b)
                            ]
                            back[k] = lax.ppermute(part, both, pairs)
                terms = [part] + [back[k] for k in sorted(back)]
                kept[ha].append((a, terms))
                kept[hb].append((b, terms))
                continue
            for h, plan in ((ha, chain_levels), (hb, tree_levels)):
                top = len(plan(0, nz)) - 1
                sides = []
                for i in (0, 1):
                    part = product(got[a, h], i * tall, (i + 1) * tall)
                    terms = climbed(part, a, top, plan)
                    sent = add(terms).astype(jnp.float16)
                    late[i][h].append(lax.ppermute(sent, both, rise(a, top, i, plan)))
                    sides.append(terms)
                kept[h].append((a, sides))

        def owned(m):
            terms = [dict(kept[h])[m] for h in (0, 1)]

            def branch():
                pieces = []
                for i in (0, 1):
                    for values in terms:
                        if isinstance(values[0], list):
                            values = values[i]
                        else:
                            values = [v[:, i * tall : (i + 1) * tall] for v in values]
                        pieces.append(add(values))
                return pieces

            return branch

        pieces = lax.switch(mine, [owned(m) for m in range(chips)])
        pieces = pieces[:2] + [lax.ppermute(pieces[2 + h], "feat", hop(1)) for h in (0, 1)]
        pieces = [add([v] + late[j // 2][j % 2]) for j, v in enumerate(pieces)]
        scales = 1 / (jnp.sqrt(jnp.float32(frames) - jnp.array(LAGS, jnp.float32)) * room)
        return finished(core, scales[:, None, None] * grow, across.reshape(1, 2 * cols), pieces)

    return shards


def plain(trajectory):
    rows = trajectory.shape[0]
    frames = rows * lax.axis_size("tm")
    mean = lax.psum(jnp.sum(trajectory, axis=0), "tm") / frames
    centered = (trajectory - mean).astype(jnp.bfloat16)
    gathered = lax.all_gather(centered, "feat", axis=1, tiled=True)
    steps = [(i, i - 1) for i in range(1, lax.axis_size("tm"))]
    tail = lax.ppermute(gathered[:HALO], "tm", steps)
    extended = jnp.concatenate([gathered, tail], axis=0)
    blocks = [
        lax.dot_general(
            centered,
            extended[lag : lag + rows],
            (((0,), (0,)), ((), ())),
            preferred_element_type=jnp.float32,
        )
        for lag in LAGS
    ]
    summed = lax.psum_scatter(jnp.stack(blocks), "tm", scatter_dimension=2, tiled=True)
    scales = jnp.sqrt(jnp.float32(frames) - jnp.array(LAGS, jnp.float32))
    return summed / scales[:, None, None]


def solution(mesh):
    nz, nf = mesh.shape["tm"], mesh.shape["feat"]
    paired = nf == 2 * nz and nz & (nz - 1) == 0 and nz > 2
    body = make(mesh) if paired else plain

    return jax.shard_map(
        body,
        mesh=mesh,
        in_specs=(P("tm", "feat"),),
        out_specs=P(None, "feat", "tm"),
        check_vma=False,
    )
```

```python
import math

import jax
import jax.numpy as jnp
from jax import lax
from jax.experimental import pallas as pl
from jax.experimental.pallas import tpu as pltpu
from jax.sharding import PartitionSpec as P


LAGS = (0, 1, 4, 16)
HALO = max(LAGS)


def bits(mask):
    return [b for b in range(mask.bit_length()) if mask >> b & 1]


def last_hop(mask, half):
    return bits(mask)[-1] if half == 0 else bits(mask)[0]


def arrivals(chips):
    singles = [m for m in range(1, chips) if len(bits(m)) == 1]
    order = [(m, i % 2) for i, m in enumerate(singles)]
    order += [(m, 1 - i % 2) for i, m in enumerate(singles)]
    if len(singles) % 2:
        order = [(m, h) for m in singles for h in (0, 1)]
    several = [m for m in range(1, chips) if len(bits(m)) > 1]
    order += [(m, h) for m in sorted(several, key=lambda m: len(bits(m))) for h in (0, 1)]
    return [order[i : i + 2] for i in range(0, len(order), 2)]


def tree_levels(q, count):
    def rep(low, size):
        if low <= q < low + size:
            return q
        return low + size - 1 if low + size <= q else low

    levels, size = [], 2
    while size <= count:
        moves = []
        for low in range(0, count, size):
            target = rep(low, size)
            a, b = rep(low, size // 2), rep(low + size // 2, size // 2)
            moves.append((a if target == b else b, target))
        levels.append(moves)
        size *= 2
    return levels


def chain_levels(q, count):
    return [
        [(k, k + 1)] * (k < q) + [(count - 1 - k, count - 2 - k)] * (count - 1 - k > q)
        for k in range(count - 1)
    ]


def lagged_kernel(*refs):
    out_ref, wide_ref, exact_ref = refs[-3:]
    rows, cols = wide_ref.shape[0] - HALO, wide_ref.shape[1]
    half = cols // 2
    step = pl.program_id(0)
    here = pl.ds(pl.multiple_of(step * rows, rows), rows)
    for i in (0, 1):
        first_ref, *parts = refs[5 * i : 5 * i + 5]
        for h in (0, 1):
            main_ref, prior_ref = parts[2 * h : 2 * h + 2]
            columns = slice(h * half, (h + 1) * half)
            prior = jnp.where(step == 0, first_ref[:, columns], prior_ref[...])
            exact_ref[:HALO, columns] = prior
            exact_ref[HALO:, columns] = main_ref[...]
            wide_ref[:HALO, columns] = prior.astype(jnp.float32)
            wide_ref[HALO:, columns] = main_ref[...].astype(jnp.float32)
        for k, lag in enumerate(LAGS):
            start = HALO - lag
            source = exact_ref if start % 16 == 0 else wide_ref
            at = (len(LAGS) * i + k) * cols
            out_ref[here, at : at + cols] = source[start : start + rows].astype(out_ref.dtype)


def lagged_columns(own, other):
    rows, half = own[1].shape
    cols = 2 * half
    step = math.gcd(rows, 512)
    wide = 2 * len(LAGS) * cols
    first = pl.BlockSpec((HALO, cols), lambda i: (0, 0))
    main = pl.BlockSpec((step, half), lambda i: (i, 0))
    prior = pl.BlockSpec((HALO, half), lambda i: (jnp.maximum(i * (step // HALO) - 1, 0), 0))
    operands = [v for before, a, b in (own, other) for v in (before, a, a, b, b)]
    return pl.pallas_call(
        lagged_kernel,
        out_shape=pltpu.VMEM((rows, wide), own[1].dtype),
        grid=(rows // step,),
        in_specs=[first, main, prior, main, prior] * 2,
        out_specs=pl.BlockSpec(memory_space=pltpu.VMEM),
        scratch_shapes=[
            pltpu.VMEM((step + HALO, cols), jnp.float32),
            pltpu.VMEM((step + HALO, cols), own[1].dtype),
        ],
        cost_estimate=pl.CostEstimate(
            flops=rows * wide, bytes_accessed=2 * rows * (wide + 2 * cols), transcendentals=0
        ),
        compiler_params=pltpu.CompilerParams(vmem_limit_bytes=16 * 1024 * 1024),
        name="lagged",
    )(*operands)


def join_kernel(left_ref, right_ref, out_ref, sems):
    cols = left_ref.shape[1]
    copies = [
        pltpu.make_async_copy(ref, out_ref.at[:, i * cols : (i + 1) * cols], sems.at[i])
        for i, ref in enumerate((left_ref, right_ref))
    ]
    for copy in copies:
        copy.start()
    for copy in copies:
        copy.wait()


def joined(left, right):
    rows, cols = left.shape
    anywhere = pl.BlockSpec(memory_space=pl.ANY)
    if cols % 128:
        return jnp.concatenate([left, right], 1)
    return pl.pallas_call(
        join_kernel,
        out_shape=pltpu.VMEM((rows, 2 * cols), left.dtype),
        in_specs=[anywhere, anywhere],
        out_specs=pl.BlockSpec(memory_space=pltpu.VMEM),
        scratch_shapes=[pltpu.SemaphoreType.DMA((2,))],
        cost_estimate=pl.CostEstimate(flops=0, bytes_accessed=8 * rows * cols, transcendentals=0),
        compiler_params=pltpu.CompilerParams(vmem_limit_bytes=1024 * 1024),
        name="join",
    )(left, right)


def order_kernel(flag_ref, a_ref, b_ref, lead_ref, rest_ref, sems):
    def copied(lead, rest):
        copies = [
            pltpu.make_async_copy(lead, lead_ref, sems.at[0]),
            pltpu.make_async_copy(rest, rest_ref, sems.at[1]),
        ]
        for copy in copies:
            copy.start()
        for copy in copies:
            copy.wait()

    @pl.when(flag_ref[0] == 1)
    def _():
        copied(a_ref, b_ref)

    @pl.when(flag_ref[0] != 1)
    def _():
        copied(b_ref, a_ref)


def ordered(flag, a, b):
    anywhere = pl.BlockSpec(memory_space=pl.ANY)
    return pl.pallas_call(
        order_kernel,
        out_shape=[pltpu.VMEM(a.shape, a.dtype)] * 2,
        in_specs=[pl.BlockSpec(memory_space=pltpu.SMEM), anywhere, anywhere],
        out_specs=[pl.BlockSpec(memory_space=pltpu.VMEM)] * 2,
        scratch_shapes=[pltpu.SemaphoreType.DMA((2,))],
        cost_estimate=pl.CostEstimate(
            flops=0, bytes_accessed=8 * a.shape[0] * a.shape[1], transcendentals=0
        ),
        compiler_params=pltpu.CompilerParams(vmem_limit_bytes=1024 * 1024),
        name="order",
    )(flag.astype(jnp.int32)[None], a, b)


def finish_kernel(core_ref, rows_ref, across_ref, *refs):
    out_ref = refs[-1]
    half = refs[0].shape[0]
    for i in (0, 1):
        owner = core_ref[0] if i == 0 else 1 - core_ref[0]
        for h in (0, 1):
            at = pl.ds(pl.multiple_of((2 * owner + h) * half, half), half)
            value = (refs[2 * i + h][...] * rows_ref[0]).T
            out_ref[0, :, at] = value * across_ref[:, at]


def finished(core, rows, across, pieces):
    lags, _, tall = rows.shape
    half = pieces[0].shape[0]
    wide = 4 * half
    if half % 128:
        order = lambda i: [jnp.where(core == i, pieces[h], pieces[2 + h]) for h in (0, 1)]
        value = jnp.concatenate(order(0) + order(1)).T.reshape(lags, tall, wide)
        return value * rows.transpose(0, 2, 1) * across
    return pl.pallas_call(
        finish_kernel,
        out_shape=jax.ShapeDtypeStruct((lags, tall, wide), jnp.float32),
        grid=(lags,),
        in_specs=[
            pl.BlockSpec(memory_space=pltpu.SMEM),
            pl.BlockSpec((1, 1, tall), lambda k: (k, 0, 0)),
            pl.BlockSpec((1, wide), lambda k: (0, 0)),
        ]
        + [pl.BlockSpec((half, tall), lambda k: (0, k))] * 4,
        out_specs=pl.BlockSpec((1, tall, wide), lambda k: (k, 0, 0)),
        cost_estimate=pl.CostEstimate(
            flops=2 * lags * tall * wide, bytes_accessed=8 * lags * tall * wide, transcendentals=0
        ),
        compiler_params=pltpu.CompilerParams(vmem_limit_bytes=16 * 1024 * 1024),
        name="finish",
    )(core[None], rows, across, *pieces)


def make(mesh):
    nz, nf = mesh.shape["tm"], mesh.shape["feat"]
    chips = nf // 2
    levels = nz.bit_length() - 1

    def shards(trajectory):
        rows, cols = trajectory.shape
        half = cols // 2
        tall = len(LAGS) * cols
        frames = rows * nz
        z, f = lax.axis_index("tm"), lax.axis_index("feat")
        chip, core = lax.div(f, 2), lax.rem(f, 2)
        mine = lax.bitwise_xor(chip, z)
        room = 2.0 ** math.floor(math.log2(32768.0 / frames))

        def hop(mask):
            return [(i, i ^ mask) for i in range(nf)]

        stats = jnp.stack([jnp.sum(trajectory, 0), jnp.max(trajectory, 0), jnp.min(trajectory, 0)])
        others = [
            lax.ppermute(stats, "tm", [(i, i ^ k) for i in range(nz)])
            for k in reversed(range(1, nz))
        ]
        total, high, low = stats
        for other in others:
            total = total + other[0]
            high, low = jnp.maximum(high, other[1]), jnp.minimum(low, other[2])
        mean = total / frames
        spread = high - low + jnp.maximum(jnp.abs(high), jnp.abs(low)) * 2.0**-14
        power = jnp.ceil(jnp.log2(jnp.maximum(spread, 2.0**-60)))
        shrink = lax.reduce_precision(jnp.exp2(-power), 8, 7)
        grow = lax.reduce_precision(jnp.exp2(power), 8, 7)

        def centre(value, low=0, high=cols):
            return ((value - mean[low:high]) * shrink[low:high]).astype(jnp.bfloat16)

        got = {}
        for h in (0, 1):
            low, high = h * half, (h + 1) * half
            got[0, h] = centre(trajectory[:, low:high], low, high)
            mean, shrink, got[0, h] = lax.optimization_barrier((mean, shrink, got[0, h]))
        slots = arrivals(chips)
        for slot in slots:
            for m, h in slot:
                if len(bits(m)) == 1:
                    got[m, h] = lax.ppermute(got[0, h], "feat", hop(2 * m))

        swapped = [lax.ppermute(got[0, h], "feat", hop(1)) for h in (0, 1)]
        tail, got[0, 1] = lax.optimization_barrier((trajectory, got[0, 1]))
        before = lax.ppermute(tail[rows - HALO :], "tm", [(i, i + 1) for i in range(nz - 1)])
        first = jnp.where(z == 0, jnp.bfloat16(0), centre(before))
        lagged = lagged_columns(
            (first, got[0, 0], got[0, 1]), (lax.ppermute(first, "feat", hop(1)), *swapped)
        )

        turned = lax.ppermute(grow[None], "feat", hop(1))[0]
        pair = jnp.stack([jnp.where(core == 0, grow, turned), jnp.where(core == 0, turned, grow)])
        across = pair
        for m in range(1, chips):
            across = jnp.where(mine == m, lax.ppermute(pair, "feat", hop(2 * m)), across)

        def product(block, low=0, high=2 * tall):
            value = lax.dot_general(
                block,
                lagged[:, low:high],
                (((0,), (0,)), ((), ())),
                preferred_element_type=jnp.float32,
            )
            return (value * room).astype(jnp.float16)

        def wide(value):
            return value.astype(jnp.float32)

        def rise(mask, level, flip=0, plan=tree_levels):
            return [
                (x * nf + j, y * nf + (j ^ flip))
                for j in range(nf)
                for x, y in plan(j // 2 ^ mask, nz)[level]
            ]

        both = ("tm", "feat")
        top = levels - 1
        none = jnp.float32(0)

        def add(values):
            total = wide(values[0])
            for value in values[1:]:
                total = total + wide(value)
            return total

        def climbed(part, mask, until, plan=tree_levels):
            terms = [part]
            for level in range(until):
                sent = part if level == 0 else add(terms).astype(jnp.float16)
                terms.append(lax.ppermute(sent, both, rise(mask, level, 0, plan)))
            return terms

        part = product(joined(got[0, 0], got[0, 1]))
        terms = climbed(part, 0, top)
        terms.append(lax.ppermute(add(terms).astype(jnp.float16), both, rise(0, top)))
        kept = [[(0, [v[h * half : (h + 1) * half] for v in terms])] for h in (0, 1)]

        for slot in slots:
            for m, h in slot:
                if len(bits(m)) > 1:
                    axis = 1 << last_hop(m, h)
                    got[m, h] = lax.ppermute(got[m ^ axis, h], "feat", hop(2 * axis))

        late = [[[], []], [[], []]]
        for slot in slots:
            (a, ha), (b, hb) = slot
            if a != b:
                low = (a ^ b) & -(a ^ b)
                flag = lax.bitwise_and(lax.bitwise_xor(mine, a), low) != 0
                blocks = ordered(flag, got[a, ha], got[b, hb])
                back = {}
                for leading, block in ((True, blocks[0]), (False, blocks[1])):
                    part = product(block)
                    for k in range(1, nz):
                        if bool(k & low) == leading:
                            pairs = [
                                (y * nf + i, (y ^ k) * nf + i)
                                for i in range(nf)
                                for y in range(nz)
                                if i // 2 ^ y ^ k in (a, b)
                            ]
                            back[k] = lax.ppermute(part, both, pairs)
                terms = [part] + [back[k] for k in sorted(back)]
                kept[ha].append((a, terms))
                kept[hb].append((b, terms))
                continue
            for h in (ha, hb):
                sides = []
                for i in (0, 1):
                    plan = chain_levels if (h, i) == (ha, 0) else tree_levels
                    top = len(plan(0, nz)) - 1
                    part = product(got[a, h], i * tall, (i + 1) * tall)
                    terms = climbed(part, a, top, plan)
                    sent = add(terms).astype(jnp.float16)
                    late[i][h].append(lax.ppermute(sent, both, rise(a, top, i, plan)))
                    sides.append(terms)
                kept[h].append((a, sides))

        def owned(m):
            terms = [dict(kept[h])[m] for h in (0, 1)]

            def branch():
                pieces = []
                for i in (0, 1):
                    for values in terms:
                        if isinstance(values[0], list):
                            values = values[i]
                        else:
                            values = [v[:, i * tall : (i + 1) * tall] for v in values]
                        pieces.append(add(values))
                return pieces

            return branch

        pieces = lax.switch(mine, [owned(m) for m in range(chips)])
        pieces = pieces[:2] + [lax.ppermute(pieces[2 + h], "feat", hop(1)) for h in (0, 1)]
        pieces = [add([v] + late[j // 2][j % 2]) for j, v in enumerate(pieces)]
        scales = 1 / (jnp.sqrt(jnp.float32(frames) - jnp.array(LAGS, jnp.float32)) * room)
        return finished(core, scales[:, None, None] * grow, across.reshape(1, 2 * cols), pieces)

    return shards


def plain(trajectory):
    rows = trajectory.shape[0]
    frames = rows * lax.axis_size("tm")
    mean = lax.psum(jnp.sum(trajectory, axis=0), "tm") / frames
    centered = (trajectory - mean).astype(jnp.bfloat16)
    gathered = lax.all_gather(centered, "feat", axis=1, tiled=True)
    steps = [(i, i - 1) for i in range(1, lax.axis_size("tm"))]
    tail = lax.ppermute(gathered[:HALO], "tm", steps)
    extended = jnp.concatenate([gathered, tail], axis=0)
    blocks = [
        lax.dot_general(
            centered,
            extended[lag : lag + rows],
            (((0,), (0,)), ((), ())),
            preferred_element_type=jnp.float32,
        )
        for lag in LAGS
    ]
    summed = lax.psum_scatter(jnp.stack(blocks), "tm", scatter_dimension=2, tiled=True)
    scales = jnp.sqrt(jnp.float32(frames) - jnp.array(LAGS, jnp.float32))
    return summed / scales[:, None, None]


def solution(mesh):
    nz, nf = mesh.shape["tm"], mesh.shape["feat"]
    paired = nf == 2 * nz and nz & (nz - 1) == 0 and nz > 2
    body = make(mesh) if paired else plain

    return jax.shard_map(
        body,
        mesh=mesh,
        in_specs=(P("tm", "feat"),),
        out_specs=P(None, "feat", "tm"),
        check_vma=False,
    )
```
